32 devices in a mesh: row: 8 (over y, x, core), col: 4 (over z).
Axes of the slice: x: 2, y: 2, z: 4, core: 2. Of those that a mesh axis runs over, the one named last changes fastest.
Arguments:
- fac_ac: bfloat16 [768, 12, 256], P('row', 'col'), may hold values from -1.5 to 1.5
- fac_bd: bfloat16 [768, 24, 256], P('col', 'row'), may hold values from -1.5 to 1.5
- amps: bfloat16 [12, 24, 128], P('col', 'row'), may hold values from -0.375 to 0.375
Outputs:
- ladder: float32 [768, 768, 128], P('row', 'col')
The draws below stay inside these ranges and needn't reach their ends.
All inputs are finite; a program needn't handle non-finite values.
Results may differ from the reference program's by a relative error of at most 0.0029.
Values may be sent and summed in bfloat16 or wider, within the bound.
No kernel may reach another device: no remote copies, remote signals or barrier semaphores. Data moves between devices by JAX's collectives and lax.ppermute only.
A program may use at most 64 MiB of HBM per device.

```python
import jax
import jax.numpy as jnp
from jax import lax

V = 768
Q = 256
PAIRS = 128
C_DEV = 3
D_DEV = 3
CW = 12
DW = 24
N_ROW = 8
N_COL = 4


def level_of(rng, shape, shards, least, largest):
    level = 1.0
    for dim, blocks in shards:
        draws = jax.random.uniform(jax.random.fold_in(jax.random.fold_in(rng, 6), dim), (blocks,), jnp.float32, least / len(shards), largest / len(shards))
        level = level * jnp.repeat(jnp.exp(draws), shape[dim] // blocks).reshape((-1,) + (1,) * (len(shape) - 1 - dim))
    return level


def noise(key, shape, spread, bound, split=(), kind=jnp.bfloat16):
    entries = spread * jax.random.normal(key, shape, jnp.float32)
    if split:
        entries = entries * level_of(key, shape, split, -0.22, 0.18)
    return jnp.clip(entries, -bound, bound).astype(kind)


def setup_inputs(seed: int = 0) -> dict:
    arg_keys = jax.random.split(jax.random.key(seed), 4)
    return {
        "fac_ac": noise(arg_keys[0], (V, CW, Q), (Q // 16) ** -0.5, 1.5, ((0, 8), (1, 4))),
        "fac_bd": noise(arg_keys[1], (V, DW, Q), (Q // 16) ** -0.5, 1.5, ((0, 4), (1, 8))),
        "amps": noise(arg_keys[2], (CW, DW, PAIRS), (C_DEV * N_COL * D_DEV * N_ROW) ** -0.5, 0.375, ((0, 4), (1, 8))),
    }


def reference(fac_ac, fac_bd, amps):
    bd_full = fac_bd.astype(jnp.float32)
    amp_full = amps.astype(jnp.float32)

    def one_block(ac_block):
        ints = jnp.einsum("acq,bdq->acbd", ac_block.astype(jnp.float32), bd_full, precision=lax.Precision.HIGHEST)
        ints = lax.optimization_barrier(ints.astype(jnp.bfloat16)).astype(jnp.float32)
        return jnp.einsum("cdp,acbd->abp", amp_full, ints, precision=lax.Precision.HIGHEST)

    blocks = fac_ac.reshape(V // 16, 16, fac_ac.shape[1], fac_ac.shape[2])
    parts = lax.map(one_block, blocks)
    return parts.reshape(V, V, amps.shape[2])
```

```python
import functools

import jax
import jax.numpy as jnp
from jax import lax
from jax.experimental import pallas as pl
from jax.experimental.pallas import tpu as pltpu
from jax.sharding import PartitionSpec as P

BF16, F32 = jnp.bfloat16, jnp.float32


def rounded_up(n, k):
    return -(-n // k) * k


def kernel(m_count, s_count, *refs):
    bd_refs, ac_refs = refs[:m_count], refs[m_count : m_count + s_count]
    amp_ref, out_ref, ints_ref, amp_rows = refs[m_count + s_count :]
    c_dev, ta, q = ac_refs[0].shape
    d_dev, nb, _ = bd_refs[0].shape
    c_all = c_dev * s_count
    c_pad = rounded_up(c_all, 16)

    @pl.when(pl.program_id(0) == 0)
    def _():
        _, s, slots, pairs = amp_ref.shape
        shape = (d_dev * c_pad, s * slots)
        to, at = (lax.broadcasted_iota(jnp.int32, shape, i) for i in (0, 1))
        d, c = to // c_pad, to % c_pad
        source = (c // c_dev) * slots + (c % c_dev) * d_dev + d
        pick = jnp.where((at == source) & (c < c_all), 1.0, 0.0).astype(BF16)
        for m in range(m_count):
            rows = jnp.dot(pick, amp_ref[m].reshape(s * slots, pairs), preferred_element_type=F32)
            amp_rows[m * d_dev * c_pad : (m + 1) * d_dev * c_pad, :] = rows.astype(BF16)

    shape = (ta * c_pad, c_dev * ta)
    to, at = (lax.broadcasted_iota(jnp.int32, shape, i) for i in (0, 1))
    left = jnp.zeros((ta * c_pad, q), F32)
    for s in range(s_count):
        pick = (to % c_pad == at // ta + s * c_dev) & (to // c_pad == at % ta)
        pick = jnp.where(pick, 1.0, 0.0).astype(BF16)
        left += jnp.dot(pick, ac_refs[s][...].reshape(c_dev * ta, q), preferred_element_type=F32)
    left = left.astype(BF16)
    for m in range(m_count):
        for i in range(d_dev):
            ints = lax.dot_general(
                left, bd_refs[m][i], (((1,), (1,)), ((), ())), preferred_element_type=F32
            )
            k = (m * d_dev + i) * c_pad
            ints_ref[:, k : k + c_pad, :] = ints.astype(BF16).reshape(ta, c_pad, nb)
    for a in range(ta):
        out_ref[a] = lax.dot_general(
            ints_ref[a], amp_rows[...], (((0,), (0,)), ((), ())), preferred_element_type=F32
        )


def ladder(bd_pieces, ac_pieces, amps):
    c_dev, na, q = ac_pieces[0].shape
    d_dev, nb, _ = bd_pieces[0].shape
    m_count, s_count, pairs = len(bd_pieces), len(ac_pieces), amps.shape[-1]
    ta = 16 if na % 16 == 0 else 8
    depth = m_count * d_dev * rounded_up(c_dev * s_count, 16)
    whole = pl.Buffered(1)
    in_specs = (
        [pl.BlockSpec((d_dev, nb, q), lambda i: (0, 0, 0), pipeline_mode=whole)] * m_count
        + [pl.BlockSpec((c_dev, ta, q), lambda i: (0, i, 0))] * s_count
        + [pl.BlockSpec(amps.shape, lambda i: (0, 0, 0, 0), pipeline_mode=whole)]
    )
    return pl.pallas_call(
        functools.partial(kernel, m_count, s_count),
        grid=(na // ta,),
        in_specs=in_specs,
        out_specs=pl.BlockSpec((ta, nb, pairs), lambda i: (i, 0, 0)),
        out_shape=jax.ShapeDtypeStruct((na, nb, pairs), F32),
        scratch_shapes=[pltpu.VMEM((ta, depth, nb), BF16), pltpu.VMEM((depth, pairs), BF16)],
        compiler_params=pltpu.CompilerParams(vmem_limit_bytes=60 << 20),
    )(*bd_pieces, *ac_pieces, amps)


def body(n_row, n_col, fac_ac, fac_bd, amps):
    def flip(x, mask):
        return lax.ppermute(x, "row", [(i, i ^ mask) for i in range(n_row)])

    def shift(x, s):
        return lax.ppermute(x, "col", [(i, (i + s) % n_col) for i in range(n_col)])

    bd = jnp.transpose(fac_bd, (1, 0, 2))
    ac = jnp.transpose(fac_ac, (1, 0, 2))
    c_dev, d_dev, pairs = amps.shape
    slots = rounded_up(c_dev * d_dev, 16)
    own = jnp.pad(amps.reshape(c_dev * d_dev, pairs), ((0, slots - c_dev * d_dev), (0, 0)))

    bd_even = [bd if m == 0 else flip(bd, m) for m in range(0, n_row, 2)]
    bd_pieces = [x for even in bd_even for x in (even, flip(even, 1))]
    ac_pieces = [ac if s == 0 else shift(ac, s) for s in range(n_col)]
    gathered = jnp.stack([own if s == 0 else shift(own, s) for s in range(n_col)])[None]
    bit = 1
    while bit < n_row:
        gathered = jnp.concatenate([gathered, flip(gathered, bit)])
        bit *= 2
    return ladder(bd_pieces, ac_pieces, gathered)


def solution(mesh):
    n_row, n_col = mesh.shape["row"], mesh.shape["col"]
    in_specs = (P("row", "col", None), P("col", "row", None), P("col", "row", None))
    out_specs = P("row", "col", None)
    return jax.shard_map(
        functools.partial(body, n_row, n_col),
        mesh=mesh, in_specs=in_specs, out_specs=out_specs, check_vma=False,
    )
```

```python
import functools

import jax
import jax.numpy as jnp
from jax import lax
from jax.experimental import pallas as pl
from jax.experimental.pallas import tpu as pltpu
from jax.sharding import PartitionSpec as P


BF16, F32 = jnp.bfloat16, jnp.float32


def rounded_up(n, k):
    return -(-n // k) * k


def one_hot(shape, source):
    to, at = (lax.broadcasted_iota(jnp.int32, shape, k) for k in (0, 1))
    return jnp.where(source(to, at), 1.0, 0.0).astype(BF16)


def plain_kernel(m_count, s_count, *refs):
    bd_refs, refs = refs[:m_count], refs[m_count:]
    ac_refs, refs = refs[:s_count], refs[s_count:]
    amp_refs, (out_ref, ints_ref, amp_rows) = refs[:m_count], refs[m_count:]
    c_dev, ta, q = ac_refs[0].shape
    d_dev, nb, _ = bd_refs[0].shape
    c_pad = rounded_up(c_dev * s_count, 16)

    @pl.when(pl.program_id(0) == 0)
    def _():
        for m in range(m_count):
            amp_rows[m * d_dev * c_pad : (m + 1) * d_dev * c_pad, :] = amp_refs[m][...]

    left = jnp.zeros((ta * c_pad, q), F32)
    for s in range(s_count):
        pick = one_hot(
            (ta * c_pad, c_dev * ta),
            lambda to, at: (to % c_pad == at // ta + s * c_dev) & (to // c_pad == at % ta),
        )
        left += jnp.dot(pick, ac_refs[s][...].reshape(c_dev * ta, q), preferred_element_type=F32)
    left = left.astype(BF16)
    for d in range(m_count * d_dev):
        ints = lax.dot_general(
            left, bd_refs[d // d_dev][d % d_dev], (((1,), (1,)), ((), ())),
            preferred_element_type=F32,
        )
        ints_ref[:, d * c_pad : (d + 1) * c_pad, :] = ints.astype(BF16).reshape(ta, c_pad, nb)
    for a in range(ta):
        out_ref[a] = lax.dot_general(
            ints_ref[a], amp_rows[...], (((0,), (0,)), ((), ())), preferred_element_type=F32
        )


def kernel(m_count, s_count, blocks, *refs):
    bd_refs, refs = refs[:m_count], refs[m_count:]
    ac_refs, refs = refs[:s_count], refs[s_count:]
    amp_refs, refs = refs[:m_count], refs[m_count:]
    out_ref, ints_a, ints_b, amp_in, amp_rows, picks = refs
    c_dev, _, q = ac_refs[0].shape
    d_dev, nb, _ = bd_refs[0].shape
    ta, half = out_ref.shape[0], out_ref.shape[0] // 2
    step = amp_refs[0].shape[0]
    c_pad = step // d_dev
    groups = m_count * d_dev // 4
    i = pl.program_id(0)

    def prepare():
        odd = lax.axis_index("row") % 2
        for m in range(m_count):
            at = jnp.where(odd == 1, 7 - m, m) if 2 <= m < 6 else m
            amp_in[pl.ds(pl.multiple_of(at * step, 16), step), :] = amp_refs[m][...]

        def amp_source(skip, swap):
            def source(to, at):
                j = jnp.where(to < 32, to // 8, ((to - 32) // 4) ^ swap)
                c = jnp.where(to < 32, to % 8, 8 + to % 4)
                return at == (skip + j) * c_pad + c

            return source

        amp_picks = {}
        for g in range(groups):
            piece, skip = divmod(4 * g, d_dev)
            rows = amp_in[piece * step : (piece + 2) * step, :]
            for swap in (0, 1):
                if (skip, swap) not in amp_picks:
                    amp_picks[skip, swap] = one_hot((48, 2 * step), amp_source(skip, swap))
                picked = jnp.dot(amp_picks[skip, swap], rows, preferred_element_type=F32)
                amp_rows[swap, g * 48 : (g + 1) * 48, :] = picked.astype(BF16)

        def left_source(to, at):
            slot, low = to // 8, to - 8 * ta
            pair, j = (low % (8 * half)) // 8, low % 8
            crossed = jnp.where(low < 8 * half, 0, 1)
            a = jnp.where(low < 0, 2 * (slot % half) + slot // half, 2 * pair + ((j // 4) ^ crossed))
            c = jnp.where(low < 0, to % 8, 8 + j % 4)
            return at == c * ta + a

        picks[...] = one_hot(picks.shape, left_source)

    def left_rows():
        at = pl.ds(pl.multiple_of(jnp.minimum(i, blocks - 1) * ta, ta), ta)
        rows = jnp.concatenate([ac[:, at, :].reshape(c_dev * ta, q) for ac in ac_refs])
        rows = jnp.dot(picks[...], rows, preferred_element_type=F32).astype(BF16)
        high, even, odd = rows[: 8 * ta], rows[8 * ta : 8 * (ta + half)], rows[8 * (ta + half) :]
        return jnp.concatenate([high, even]), jnp.concatenate([high, odd])

    upper = lax.broadcasted_iota(jnp.int32, (half, 8, nb), 1) < 4

    def first(left, ints_ref, g):
        high, low = [], []
        for d in range(4 * g, 4 * g + 4):
            ints = lax.dot_general(
                left[d % 2], bd_refs[d // d_dev][d % d_dev], (((1,), (1,)), ((), ())),
                preferred_element_type=F32,
            )
            high.append(ints[: 8 * ta].reshape(ta, 8, nb))
            low.append(ints[8 * ta :].reshape(half, 8, nb))
        k = 48 * g
        for n in (0, 2):
            both = jnp.concatenate(high[n : n + 2], axis=1).astype(BF16)
            ints_ref[:, k + 8 * n : k + 8 * n + 16, :] = both
        even = [jnp.where(upper, low[n], low[n + 1]) for n in (0, 2)]
        odd = [jnp.where(upper, low[n + 1], low[n]) for n in (0, 2)]
        ints_ref[:half, k + 32 : k + 48, :] = jnp.concatenate(even, axis=1).astype(BF16)
        ints_ref[half:, k + 32 : k + 48, :] = jnp.concatenate(odd, axis=1).astype(BF16)

    def second(ints_ref, slot):
        out_ref[2 * (slot % half) + slot // half] = lax.dot_general(
            ints_ref[slot], amp_rows[slot // half], (((0,), (0,)), ((), ())),
            preferred_element_type=F32,
        )

    def both(done_ref, next_ref):
        left = left_rows()
        for g in range(groups):
            first(left, next_ref, g)
            for slot in range(g * ta // groups, (g + 1) * ta // groups):
                second(done_ref, slot)

    @pl.when(i == 0)
    def _():
        prepare()
        left = left_rows()
        for g in range(groups):
            first(left, ints_a, g)

    @pl.when((i % 2 == 1) & (i < blocks))
    def _():
        both(ints_a, ints_b)

    @pl.when((i % 2 == 0) & (i > 0) & (i < blocks))
    def _():
        both(ints_b, ints_a)

    @pl.when(i == blocks)
    def _():
        for slot in range(ta):
            second((ints_a, ints_b)[(blocks - 1) % 2], slot)


def ladder(bd_pieces, ac_pieces, amps):
    c_dev, na, q = ac_pieces[0].shape
    d_dev, nb, _ = bd_pieces[0].shape
    m_count, s_count, pairs = len(bd_pieces), len(ac_pieces), amps[0].shape[-1]
    ta = 16 if na % 16 == 0 else 8
    blocks = na // ta
    c_all = c_dev * s_count
    depth = m_count * d_dev * rounded_up(c_all, 16)
    if (m_count, d_dev, c_all, ta) == (8, 3, 12, 16):
        tight = m_count * d_dev * c_all
        scratch = [pltpu.VMEM((ta, tight, nb), BF16)] * 2 + [
            pltpu.VMEM((depth, pairs), BF16),
            pltpu.VMEM((2, tight, pairs), BF16),
            pltpu.VMEM((16 * ta, c_all * ta), BF16),
        ]
        body, steps, limit = functools.partial(kernel, m_count, s_count, blocks), blocks + 1, 32
        at_out = lambda i: (jnp.maximum(i - 1, 0), 0, 0)
        in_specs = [pl.BlockSpec(memory_space=pltpu.VMEM)] * (2 * m_count + s_count)
    else:
        scratch = [pltpu.VMEM((ta, depth, nb), BF16), pltpu.VMEM((depth, pairs), BF16)]
        body, steps, limit = functools.partial(plain_kernel, m_count, s_count), blocks, 60
        at_out = lambda i: (i, 0, 0)
        whole = pl.Buffered(1)
        in_specs = (
            [pl.BlockSpec((d_dev, nb, q), lambda i: (0, 0, 0), pipeline_mode=whole)] * m_count
            + [pl.BlockSpec((c_dev, ta, q), lambda i: (0, i, 0))] * s_count
            + [pl.BlockSpec(amps[0].shape, lambda i: (0, 0), pipeline_mode=whole)] * m_count
        )
    return pl.pallas_call(
        body,
        grid=(steps,),
        in_specs=in_specs,
        out_specs=pl.BlockSpec((ta, nb, pairs), at_out),
        out_shape=jax.ShapeDtypeStruct((na, nb, pairs), F32),
        scratch_shapes=scratch,
        compiler_params=pltpu.CompilerParams(vmem_limit_bytes=limit << 20),
    )(*bd_pieces, *ac_pieces, *amps)


def body(n_row, n_col, fac_ac, fac_bd, amps):
    def send(x, to):
        return lax.ppermute(x, "row", [(i, to(i)) for i in range(n_row)])

    def flip(x):
        return send(x, lambda i: i ^ 1)

    def shift(x, s):
        return lax.ppermute(x, "col", [(i, (i + s) % n_col) for i in range(n_col)])

    bd = jnp.transpose(fac_bd, (1, 0, 2))
    ac = jnp.transpose(fac_ac, (1, 0, 2))
    c_dev, d_dev, pairs = amps.shape
    c_pad = rounded_up(c_dev * n_col, 16)
    amp_cols = [amps] + [shift(amps, s) for s in range(1, n_col)]
    rows = jnp.concatenate(amp_cols)
    rows = jnp.pad(rows, ((0, c_pad - c_dev * n_col), (0, 0), (0, 0)))
    rows = jnp.transpose(rows, (1, 0, 2)).reshape(d_dev * c_pad, pairs)
    ac_pieces = [ac] + [shift(ac, s) for s in range(1, n_col)]

    def direct(x):
        pieces = []
        for m in range(0, n_row, 2):
            piece = x if m == 0 else send(x, lambda i: i ^ m)
            pieces += [piece, flip(piece)]
        return pieces

    amp_rows = direct(rows)
    if (n_row, d_dev, c_dev * n_col) != (8, 3, 12):
        return ladder(direct(bd), ac_pieces, amp_rows)

    over, then = (lambda i: i ^ (4 if i & 1 else 2)), (lambda i: i ^ (2 if i & 1 else 4))
    other = flip(bd)
    mine, its = send(bd, over), send(other, over)
    far = send(mine, then)
    bd_pieces = [flip(other), other]
    ac_pieces[0] = flip(flip(ac))
    for piece in (mine, its, far):
        bd_pieces += [piece, flip(piece)]
    order = (0, 1, 2, 5, 3, 4, 6, 7)
    amp_rows = [amp_rows[k] for k in order]
    return ladder(bd_pieces, ac_pieces, amp_rows)


def solution(mesh):
    n_row, n_col = mesh.shape["row"], mesh.shape["col"]
    in_specs = (P("row", "col", None), P("col", "row", None), P("col", "row", None))
    out_specs = P("row", "col", None)
    return jax.shard_map(
        functools.partial(body, n_row, n_col),
        mesh=mesh, in_specs=in_specs, out_specs=out_specs, check_vma=False,
    )
```

```python
import functools

import jax
import jax.numpy as jnp
from jax import lax
from jax.experimental import pallas as pl
from jax.experimental.pallas import tpu as pltpu
from jax.sharding import PartitionSpec as P


BF16, F32 = jnp.bfloat16, jnp.float32


def rounded_up(n, k):
    return -(-n // k) * k


def one_hot(shape, source):
    to, at = (lax.broadcasted_iota(jnp.int32, shape, k) for k in (0, 1))
    return jnp.where(source(to, at), 1.0, 0.0).astype(BF16)


def plain_kernel(m_count, s_count, *refs):
    bd_refs, refs = refs[:m_count], refs[m_count:]
    ac_refs, refs = refs[:s_count], refs[s_count:]
    amp_refs, (out_ref, ints_ref, amp_rows) = refs[: m_count // 2], refs[m_count // 2 :]
    c_dev, ta, q = ac_refs[0].shape
    d_dev, nb, _ = bd_refs[0].shape
    c_pad = rounded_up(c_dev * s_count, 16)

    @pl.when(pl.program_id(0) == 0)
    def _():
        step = 2 * d_dev * c_pad
        for m in range(m_count // 2):
            amp_rows[m * step : (m + 1) * step, :] = amp_refs[m][...]

    left = jnp.zeros((ta * c_pad, q), F32)
    for s in range(s_count):
        pick = one_hot(
            (ta * c_pad, c_dev * ta),
            lambda to, at: (to % c_pad == at // ta + s * c_dev) & (to // c_pad == at % ta),
        )
        left += jnp.dot(pick, ac_refs[s][...].reshape(c_dev * ta, q), preferred_element_type=F32)
    left = left.astype(BF16)
    for d in range(m_count * d_dev):
        ints = lax.dot_general(
            left, bd_refs[d // d_dev][d % d_dev], (((1,), (1,)), ((), ())),
            preferred_element_type=F32,
        )
        ints_ref[:, d * c_pad : (d + 1) * c_pad, :] = ints.astype(BF16).reshape(ta, c_pad, nb)
    for a in range(ta):
        out_ref[a] = lax.dot_general(
            ints_ref[a], amp_rows[...], (((0,), (0,)), ((), ())), preferred_element_type=F32
        )


def kernel(m_count, s_count, blocks, *refs):
    bd_refs, refs = refs[:m_count], refs[m_count:]
    ac_refs, refs = refs[:s_count], refs[s_count:]
    amp_refs, refs = refs[: m_count // 2], refs[m_count // 2 :]
    out_ref, ints_a, ints_b, amp_in, amp_rows, picks = refs
    c_dev, _, q = ac_refs[0].shape
    d_dev, nb, _ = bd_refs[0].shape
    ta, half = out_ref.shape[0], out_ref.shape[0] // 2
    step = amp_refs[0].shape[0] // 2
    c_pad = step // d_dev
    groups = m_count * d_dev // 4
    i = pl.program_id(0)

    def prepare():
        odd = lax.axis_index("row") % 2 == 1
        places = ((0, 1), (2, 5), (4, 3), (6, 7))
        swapped = (places[0], places[2], places[1], places[3])
        for amp_ref, even_at, odd_at in zip(amp_refs, places, swapped):
            for half_at in (0, 1):
                at = jnp.where(odd, odd_at[half_at], even_at[half_at]) * step
                rows = amp_ref[half_at * step : (half_at + 1) * step, :]
                amp_in[pl.ds(pl.multiple_of(at, 16), step), :] = rows

        def amp_source(skip, swap):
            def source(to, at):
                j = jnp.where(to < 32, to // 8, ((to - 32) // 4) ^ swap)
                c = jnp.where(to < 32, to % 8, 8 + to % 4)
                return at == (skip + j) * c_pad + c

            return source

        amp_picks = {}
        for g in range(groups):
            piece, skip = divmod(4 * g, d_dev)
            rows = amp_in[piece * step : (piece + 2) * step, :]
            for swap in (0, 1):
                if (skip, swap) not in amp_picks:
                    amp_picks[skip, swap] = one_hot((48, 2 * step), amp_source(skip, swap))
                picked = jnp.dot(amp_picks[skip, swap], rows, preferred_element_type=F32)
                amp_rows[swap, g * 48 : (g + 1) * 48, :] = picked.astype(BF16)

        def left_source(to, at):
            slot, low = to // 8, to - 8 * ta
            pair, j = (low % (8 * half)) // 8, low % 8
            crossed = jnp.where(low < 8 * half, 0, 1)
            a = jnp.where(low < 0, 2 * (slot % half) + slot // half, 2 * pair + ((j // 4) ^ crossed))
            c = jnp.where(low < 0, to % 8, 8 + j % 4)
            return at == c * ta + a

        picks[...] = one_hot(picks.shape, left_source)

    def left_rows():
        at = pl.ds(pl.multiple_of(jnp.minimum(i, blocks - 1) * ta, ta), ta)
        rows = jnp.concatenate([ac[:, at, :].reshape(c_dev * ta, q) for ac in ac_refs])
        rows = jnp.dot(picks[...], rows, preferred_element_type=F32).astype(BF16)
        high, even, odd = rows[: 8 * ta], rows[8 * ta : 8 * (ta + half)], rows[8 * (ta + half) :]
        return jnp.concatenate([high, even]), jnp.concatenate([high, odd])

    upper = lax.broadcasted_iota(jnp.int32, (half, 8, nb), 1) < 4

    def first(left, ints_ref, g):
        high, low = [], []
        for d in range(4 * g, 4 * g + 4):
            ints = lax.dot_general(
                left[d % 2], bd_refs[d // d_dev][d % d_dev], (((1,), (1,)), ((), ())),
                preferred_element_type=F32,
            )
            high.append(ints[: 8 * ta].reshape(ta, 8, nb))
            low.append(ints[8 * ta :].reshape(half, 8, nb))
        k = 48 * g
        for n in (0, 2):
            both = jnp.concatenate(high[n : n + 2], axis=1).astype(BF16)
            ints_ref[:, k + 8 * n : k + 8 * n + 16, :] = both
        even = [jnp.where(upper, low[n], low[n + 1]) for n in (0, 2)]
        odd = [jnp.where(upper, low[n + 1], low[n]) for n in (0, 2)]
        ints_ref[:half, k + 32 : k + 48, :] = jnp.concatenate(even, axis=1).astype(BF16)
        ints_ref[half:, k + 32 : k + 48, :] = jnp.concatenate(odd, axis=1).astype(BF16)

    def second(ints_ref, slot):
        out_ref[2 * (slot % half) + slot // half] = lax.dot_general(
            ints_ref[slot], amp_rows[slot // half], (((0,), (0,)), ((), ())),
            preferred_element_type=F32,
        )

    def both(done_ref, next_ref):
        left = left_rows()
        for g in range(groups):
            first(left, next_ref, g)
            for slot in range(g * ta // groups, (g + 1) * ta // groups):
                second(done_ref, slot)

    @pl.when(i == 0)
    def _():
        prepare()
        left = left_rows()
        for g in range(groups):
            first(left, ints_a, g)

    @pl.when((i % 2 == 1) & (i < blocks))
    def _():
        both(ints_a, ints_b)

    @pl.when((i % 2 == 0) & (i > 0) & (i < blocks))
    def _():
        both(ints_b, ints_a)

    @pl.when(i == blocks)
    def _():
        for slot in range(ta):
            second((ints_a, ints_b)[(blocks - 1) % 2], slot)


def ladder(bd_pieces, ac_pieces, amps):
    c_dev, na, q = ac_pieces[0].shape
    d_dev, nb, _ = bd_pieces[0].shape
    m_count, s_count, pairs = len(bd_pieces), len(ac_pieces), amps[0].shape[-1]
    ta = 16 if na % 16 == 0 else 8
    blocks = na // ta
    c_all = c_dev * s_count
    depth = m_count * d_dev * rounded_up(c_all, 16)
    if (m_count, d_dev, c_all, ta) == (8, 3, 12, 16):
        tight = m_count * d_dev * c_all
        scratch = [pltpu.VMEM((ta, tight, nb), BF16)] * 2 + [
            pltpu.VMEM((depth, pairs), BF16),
            pltpu.VMEM((2, tight, pairs), BF16),
            pltpu.VMEM((16 * ta, c_all * ta), BF16),
        ]
        body, steps, limit = functools.partial(kernel, m_count, s_count, blocks), blocks + 1, 32
        at_out = lambda i: (jnp.maximum(i - 1, 0), 0, 0)
        in_specs = [pl.BlockSpec(memory_space=pltpu.VMEM)] * (m_count + s_count + len(amps))
    else:
        scratch = [pltpu.VMEM((ta, depth, nb), BF16), pltpu.VMEM((depth, pairs), BF16)]
        body, steps, limit = functools.partial(plain_kernel, m_count, s_count), blocks, 60
        at_out = lambda i: (i, 0, 0)
        whole = pl.Buffered(1)
        in_specs = (
            [pl.BlockSpec((d_dev, nb, q), lambda i: (0, 0, 0), pipeline_mode=whole)] * m_count
            + [pl.BlockSpec((c_dev, ta, q), lambda i: (0, i, 0))] * s_count
            + [pl.BlockSpec(amps[0].shape, lambda i: (0, 0), pipeline_mode=whole)] * len(amps)
        )
    return pl.pallas_call(
        body,
        grid=(steps,),
        in_specs=in_specs,
        out_specs=pl.BlockSpec((ta, nb, pairs), at_out),
        out_shape=jax.ShapeDtypeStruct((na, nb, pairs), F32),
        scratch_shapes=scratch,
        compiler_params=pltpu.CompilerParams(vmem_limit_bytes=limit << 20),
    )(*bd_pieces, *ac_pieces, *amps)


def body(n_row, n_col, fac_ac, fac_bd, amps):
    def send(x, to):
        return lax.ppermute(x, "row", [(i, to(i)) for i in range(n_row)])

    def flip(x):
        return send(x, lambda i: i ^ 1)

    def shift(x, s):
        to = (lambda i: i ^ s) if n_col & (n_col - 1) == 0 else (lambda i: (i + s) % n_col)
        return lax.ppermute(x, "col", [(i, to(i)) for i in range(n_col)])

    bd = jnp.transpose(fac_bd, (1, 0, 2))
    ac = jnp.transpose(fac_ac, (1, 0, 2))
    c_dev, d_dev, pairs = amps.shape
    c_pad = rounded_up(c_dev * n_col, 16)
    amp_cols = [amps] + [shift(amps, s) for s in range(1, n_col)]
    rows = jnp.concatenate(amp_cols)
    rows = jnp.pad(rows, ((0, c_pad - c_dev * n_col), (0, 0), (0, 0)))
    rows = jnp.transpose(rows, (1, 0, 2)).reshape(d_dev * c_pad, pairs)
    ac_pieces = [ac] + [shift(ac, s) for s in range(1, n_col)]
    rows = jnp.concatenate([rows, flip(rows)])
    masks = range(2, n_row, 2)
    amp_rows = [rows] + [send(rows, lambda i: i ^ m) for m in masks]
    if (n_row, d_dev, c_dev * n_col) != (8, 3, 12):
        bd_even = [bd] + [send(bd, lambda i: i ^ m) for m in masks]
        bd_pieces = [x for even in bd_even for x in (even, flip(even))]
        return ladder(bd_pieces, ac_pieces, amp_rows)

    over, then = (lambda i: i ^ (4 if i & 1 else 2)), (lambda i: i ^ (2 if i & 1 else 4))
    other = flip(bd)
    first, second = send(bd, over), send(bd, then)
    far = send(first, then)
    bd_pieces = [flip(other), other]
    ac_pieces[0] = flip(flip(ac))
    for piece in (first, second, far):
        bd_pieces += [piece, flip(piece)]
    return ladder(bd_pieces, ac_pieces, amp_rows)


def solution(mesh):
    n_row, n_col = mesh.shape["row"], mesh.shape["col"]
    in_specs = (P("row", "col", None), P("col", "row", None), P("col", "row", None))
    out_specs = P("row", "col", None)
    return jax.shard_map(
        functools.partial(body, n_row, n_col),
        mesh=mesh, in_specs=in_specs, out_specs=out_specs, check_vma=False,
    )
```

```python
import functools

import jax
import jax.numpy as jnp
from jax import lax
from jax.experimental import pallas as pl
from jax.experimental.pallas import tpu as pltpu
from jax.sharding import PartitionSpec as P


BF16, F32 = jnp.bfloat16, jnp.float32


def rounded_up(n, k):
    return -(-n // k) * k


def one_hot(shape, source):
    to = lax.broadcasted_iota(jnp.int32, (shape[0], 1), 0)
    at = lax.broadcasted_iota(jnp.int32, (1, shape[1]), 1)
    return jnp.where(source(to, at), 1.0, 0.0).astype(BF16)


def plain_kernel(m_count, s_count, *refs):
    bd_refs, refs = refs[:m_count], refs[m_count:]
    ac_refs, refs = refs[:s_count], refs[s_count:]
    amp_refs, (out_ref, ints_ref, amp_rows) = refs[: m_count // 2], refs[m_count // 2 :]
    c_dev, ta, q = ac_refs[0].shape
    d_dev, nb, _ = bd_refs[0].shape
    c_pad = rounded_up(c_dev * s_count, 16)

    @pl.when(pl.program_id(0) == 0)
    def _():
        step = 2 * d_dev * c_pad
        for m in range(m_count // 2):
            amp_rows[m * step : (m + 1) * step, :] = amp_refs[m][...]

    left = jnp.zeros((ta * c_pad, q), F32)
    for s in range(s_count):
        pick = one_hot(
            (ta * c_pad, c_dev * ta),
            lambda to, at: (to % c_pad == at // ta + s * c_dev) & (to // c_pad == at % ta),
        )
        left += jnp.dot(pick, ac_refs[s][...].reshape(c_dev * ta, q), preferred_element_type=F32)
    left = left.astype(BF16)
    for d in range(m_count * d_dev):
        ints = lax.dot_general(
            left, bd_refs[d // d_dev][d % d_dev], (((1,), (1,)), ((), ())),
            preferred_element_type=F32,
        )
        ints_ref[:, d * c_pad : (d + 1) * c_pad, :] = ints.astype(BF16).reshape(ta, c_pad, nb)
    for a in range(ta):
        out_ref[a] = lax.dot_general(
            ints_ref[a], amp_rows[...], (((0,), (0,)), ((), ())), preferred_element_type=F32
        )


def kernel(m_count, s_count, blocks, *refs):
    bd_refs, refs = refs[:m_count], refs[m_count:]
    ac_refs, refs = refs[:s_count], refs[s_count:]
    amp_refs, refs = refs[: m_count // 2], refs[m_count // 2 :]
    out_ref, ints_a, ints_b, left_a, left_b, amp_in, amp_rows, picks = refs
    c_dev, _, q = ac_refs[0].shape
    d_dev, nb, _ = bd_refs[0].shape
    ta, half = out_ref.shape[0], out_ref.shape[0] // 2
    step = amp_refs[0].shape[0] // 2
    c_pad = step // d_dev
    groups = m_count * d_dev // 4
    i = pl.program_id(0)

    def prepare():
        odd = lax.axis_index("row") % 2 == 1
        places = ((0, 1), (2, 5), (4, 3), (6, 7))
        swapped = (places[0], places[2], places[1], places[3])
        for amp_ref, even_at, odd_at in zip(amp_refs, places, swapped):
            for half_at in (0, 1):
                at = jnp.where(odd, odd_at[half_at], even_at[half_at]) * step
                rows = amp_ref[half_at * step : (half_at + 1) * step, :]
                amp_in[pl.ds(pl.multiple_of(at, 16), step), :] = rows

        def amp_source(skip, swap):
            def source(to, at):
                j = jnp.where(to < 32, to >> 3, ((to - 32) >> 2) ^ swap)
                c = jnp.where(to < 32, to & 7, 8 + (to & 3))
                return at == (skip + j) * c_pad + c

            return source

        amp_picks = {}
        for g in range(groups):
            piece, skip = divmod(4 * g, d_dev)
            rows = amp_in[piece * step : (piece + 2) * step, :]
            for swap in (0, 1):
                if (skip, swap) not in amp_picks:
                    amp_picks[skip, swap] = one_hot((48, 2 * step), amp_source(skip, swap))
                picked = jnp.dot(amp_picks[skip, swap], rows, preferred_element_type=F32)
                amp_rows[swap, g * 48 : (g + 1) * 48, :] = picked.astype(BF16)

        def left_source(to, at):
            slot, j = to >> 3, to & 7
            pair, crossed = (slot - ta) & (half - 1), jnp.where(slot < ta + half, 0, 1)
            high = j * ta + 2 * (slot & (half - 1)) + jnp.where(slot < half, 0, 1)
            low = (8 + (j & 3)) * ta + 2 * pair + ((j >> 2) ^ crossed)
            return at == jnp.where(slot < ta, high, low)

        picks[...] = one_hot(picks.shape, left_source)

    def make_left(left_ref, block):
        at = pl.ds(pl.multiple_of(jnp.minimum(block, blocks - 1) * ta, ta), ta)
        rows = jnp.concatenate([ac[:, at, :].reshape(c_dev * ta, q) for ac in ac_refs])
        left_ref[...] = jnp.dot(picks[...], rows, preferred_element_type=F32).astype(BF16)

    def left_rows(left_ref):
        high, even = left_ref[: 8 * ta], left_ref[8 * ta : 8 * (ta + half)]
        return jnp.concatenate([high, even]), jnp.concatenate([high, left_ref[8 * (ta + half) :]])

    upper = lax.broadcasted_iota(jnp.int32, (half, 8, nb), 1) < 4

    def first(left, ints_ref, g):
        high, low = [], []
        for d in range(4 * g, 4 * g + 4):
            ints = lax.dot_general(
                left[d % 2], bd_refs[d // d_dev][d % d_dev], (((1,), (1,)), ((), ())),
                preferred_element_type=F32,
            )
            high.append(ints[: 8 * ta].reshape(ta, 8, nb))
            low.append(ints[8 * ta :].reshape(half, 8, nb))
        k = 48 * g
        for n in (0, 2):
            both = jnp.concatenate(high[n : n + 2], axis=1).astype(BF16)
            ints_ref[:, k + 8 * n : k + 8 * n + 16, :] = both
        even = [jnp.where(upper, low[n], low[n + 1]) for n in (0, 2)]
        odd = [jnp.where(upper, low[n + 1], low[n]) for n in (0, 2)]
        ints_ref[:half, k + 32 : k + 48, :] = jnp.concatenate(even, axis=1).astype(BF16)
        ints_ref[half:, k + 32 : k + 48, :] = jnp.concatenate(odd, axis=1).astype(BF16)

    def second(ints_ref, slot):
        out_ref[2 * (slot % half) + slot // half] = lax.dot_general(
            ints_ref[slot], amp_rows[slot // half], (((0,), (0,)), ((), ())),
            preferred_element_type=F32,
        )

    def both(done_ref, next_ref, left_ref, next_left):
        left = left_rows(left_ref)
        for g in range(groups):
            first(left, next_ref, g)
            if g == groups // 2:
                make_left(next_left, i + 1)
            for slot in range(g * ta // groups, (g + 1) * ta // groups):
                second(done_ref, slot)

    @pl.when(i == 0)
    def _():
        prepare()
        make_left(left_a, 0)
        left = left_rows(left_a)
        for g in range(groups):
            first(left, ints_a, g)
        make_left(left_b, 1)

    @pl.when((i % 2 == 1) & (i < blocks))
    def _():
        both(ints_a, ints_b, left_b, left_a)

    @pl.when((i % 2 == 0) & (i > 0) & (i < blocks))
    def _():
        both(ints_b, ints_a, left_a, left_b)

    @pl.when(i == blocks)
    def _():
        for slot in range(ta):
            second((ints_a, ints_b)[(blocks - 1) % 2], slot)


def ladder(bd_pieces, ac_pieces, amps):
    c_dev, na, q = ac_pieces[0].shape
    d_dev, nb, _ = bd_pieces[0].shape
    m_count, s_count, pairs = len(bd_pieces), len(ac_pieces), amps[0].shape[-1]
    ta = 16 if na % 16 == 0 else 8
    blocks = na // ta
    c_all = c_dev * s_count
    depth = m_count * d_dev * rounded_up(c_all, 16)
    if (m_count, d_dev, c_all, ta) == (8, 3, 12, 16):
        tight = m_count * d_dev * c_all
        scratch = [pltpu.VMEM((ta, tight, nb), BF16)] * 2 + [pltpu.VMEM((16 * ta, q), BF16)] * 2 + [
            pltpu.VMEM((depth, pairs), BF16),
            pltpu.VMEM((2, tight, pairs), BF16),
            pltpu.VMEM((16 * ta, c_all * ta), BF16),
        ]
        body, steps, limit = functools.partial(kernel, m_count, s_count, blocks), blocks + 1, 32
        at_out = lambda i: (jnp.maximum(i - 1, 0), 0, 0)
        in_specs = [pl.BlockSpec(memory_space=pltpu.VMEM)] * (m_count + s_count + len(amps))
    else:
        scratch = [pltpu.VMEM((ta, depth, nb), BF16), pltpu.VMEM((depth, pairs), BF16)]
        body, steps, limit = functools.partial(plain_kernel, m_count, s_count), blocks, 60
        at_out = lambda i: (i, 0, 0)
        whole = pl.Buffered(1)
        in_specs = (
            [pl.BlockSpec((d_dev, nb, q), lambda i: (0, 0, 0), pipeline_mode=whole)] * m_count
            + [pl.BlockSpec((c_dev, ta, q), lambda i: (0, i, 0))] * s_count
            + [pl.BlockSpec(amps[0].shape, lambda i: (0, 0), pipeline_mode=whole)] * len(amps)
        )
    return pl.pallas_call(
        body,
        grid=(steps,),
        in_specs=in_specs,
        out_specs=pl.BlockSpec((ta, nb, pairs), at_out),
        out_shape=jax.ShapeDtypeStruct((na, nb, pairs), F32),
        scratch_shapes=scratch,
        compiler_params=pltpu.CompilerParams(vmem_limit_bytes=limit << 20),
    )(*bd_pieces, *ac_pieces, *amps)


def body(n_row, n_col, fac_ac, fac_bd, amps):
    def send(x, to):
        return lax.ppermute(x, "row", [(i, to(i)) for i in range(n_row)])

    def flip(x):
        return send(x, lambda i: i ^ 1)

    def shift(x, s):
        to = (lambda i: i ^ s) if n_col & (n_col - 1) == 0 else (lambda i: (i + s) % n_col)
        return lax.ppermute(x, "col", [(i, to(i)) for i in range(n_col)])

    bd = jnp.transpose(fac_bd, (1, 0, 2))
    ac = jnp.transpose(fac_ac, (1, 0, 2))
    c_dev, d_dev, pairs = amps.shape
    c_pad = rounded_up(c_dev * n_col, 16)
    amp_cols = [amps] + [shift(amps, s) for s in range(1, n_col)]
    rows = jnp.concatenate(amp_cols)
    rows = jnp.pad(rows, ((0, c_pad - c_dev * n_col), (0, 0), (0, 0)))
    rows = jnp.transpose(rows, (1, 0, 2)).reshape(d_dev * c_pad, pairs)
    ac_pieces = [ac] + [shift(ac, s) for s in range(1, n_col)]
    rows = jnp.concatenate([rows, flip(rows)])
    masks = range(2, n_row, 2)
    amp_rows = [rows] + [send(rows, lambda i: i ^ m) for m in masks]
    if (n_row, d_dev, c_dev * n_col) != (8, 3, 12):
        bd_even = [bd] + [send(bd, lambda i: i ^ m) for m in masks]
        bd_pieces = [x for even in bd_even for x in (even, flip(even))]
        return ladder(bd_pieces, ac_pieces, amp_rows)

    over, then = (lambda i: i ^ (4 if i & 1 else 2)), (lambda i: i ^ (2 if i & 1 else 4))
    other = flip(bd)
    first, second = send(bd, over), send(bd, then)
    far = send(first, then)
    bd_pieces = [flip(other), other]
    ac_pieces[0] = flip(flip(ac))
    for piece in (first, second, far):
        bd_pieces += [piece, flip(piece)]
    return ladder(bd_pieces, ac_pieces, amp_rows)


def solution(mesh):
    n_row, n_col = mesh.shape["row"], mesh.shape["col"]
    in_specs = (P("row", "col", None), P("col", "row", None), P("col", "row", None))
    out_specs = P("row", "col", None)
    return jax.shard_map(
        functools.partial(body, n_row, n_col),
        mesh=mesh, in_specs=in_specs, out_specs=out_specs, check_vma=False,
    )
```

```python
import functools

import jax
import jax.numpy as jnp
from jax import lax
from jax.experimental import pallas as pl
from jax.experimental.pallas import tpu as pltpu
from jax.sharding import PartitionSpec as P


BF16, F32 = jnp.bfloat16, jnp.float32


def rounded_up(n, k):
    return -(-n // k) * k


def one_hot(shape, source):
    to = lax.broadcasted_iota(jnp.int32, (shape[0], 1), 0)
    at = lax.broadcasted_iota(jnp.int32, (1, shape[1]), 1)
    return jnp.where(source(to, at), 1.0, 0.0).astype(BF16)


def plain_kernel(m_count, s_count, *refs):
    bd_refs, refs = refs[:m_count], refs[m_count:]
    ac_refs, refs = refs[:s_count], refs[s_count:]
    amp_refs, (out_ref, ints_ref, amp_rows) = refs[: m_count // 2], refs[m_count // 2 :]
    c_dev, ta, q = ac_refs[0].shape
    d_dev, nb, _ = bd_refs[0].shape
    c_pad = rounded_up(c_dev * s_count, 16)

    @pl.when(pl.program_id(0) == 0)
    def _():
        step = 2 * d_dev * c_pad
        for m in range(m_count // 2):
            amp_rows[m * step : (m + 1) * step, :] = amp_refs[m][...]

    left = jnp.zeros((ta * c_pad, q), F32)
    for s in range(s_count):
        pick = one_hot(
            (ta * c_pad, c_dev * ta),
            lambda to, at: (to % c_pad == at // ta + s * c_dev) & (to // c_pad == at % ta),
        )
        left += jnp.dot(pick, ac_refs[s][...].reshape(c_dev * ta, q), preferred_element_type=F32)
    left = left.astype(BF16)
    for d in range(m_count * d_dev):
        ints = lax.dot_general(
            left, bd_refs[d // d_dev][d % d_dev], (((1,), (1,)), ((), ())),
            preferred_element_type=F32,
        )
        ints_ref[:, d * c_pad : (d + 1) * c_pad, :] = ints.astype(BF16).reshape(ta, c_pad, nb)
    for a in range(ta):
        out_ref[a] = lax.dot_general(
            ints_ref[a], amp_rows[...], (((0,), (0,)), ((), ())), preferred_element_type=F32
        )


def kernel(m_count, s_count, blocks, *refs):
    bd_refs, refs = refs[:m_count], refs[m_count:]
    ac_refs, refs = refs[:s_count], refs[s_count:]
    amp_refs, refs = refs[: m_count // 2], refs[m_count // 2 :]
    out_ref, ints_a, ints_b, left_a, left_b, amp_in, amp_rows, picks = refs
    c_dev, _, q = ac_refs[0].shape
    d_dev, nb, _ = bd_refs[0].shape
    ta, half = out_ref.shape[0], out_ref.shape[0] // 2
    step = amp_refs[0].shape[0] // 2
    c_pad = step // d_dev
    groups = m_count * d_dev // 4
    i = pl.program_id(0)

    def prepare():
        even = lax.axis_index("row") % 2 == 0
        places = ((0, 1), (2, 5), (4, 3), (6, 7))
        swapped = (places[0], places[2], places[1], places[3])
        for amp_ref, x_at, y_at in zip(amp_refs, places, swapped):
            for half_at in (0, 1):
                at = jnp.where(even, y_at[half_at], x_at[half_at]) * step
                rows = amp_ref[half_at * step : (half_at + 1) * step, :]
                amp_in[pl.ds(pl.multiple_of(at, 16), step), :] = rows

        def amp_source(skip, swap):
            def source(to, at):
                j = jnp.where(to < 32, to >> 3, ((to - 32) >> 2) ^ swap)
                c = jnp.where(to < 32, to & 7, 8 + (to & 3))
                return at == (skip + j) * c_pad + c

            return source

        amp_picks = {}
        for g in range(groups):
            piece, skip = divmod(4 * g, d_dev)
            rows = amp_in[piece * step : (piece + 2) * step, :]
            for swap in (0, 1):
                if (skip, swap) not in amp_picks:
                    amp_picks[skip, swap] = one_hot((48, 2 * step), amp_source(skip, swap))
                picked = jnp.dot(amp_picks[skip, swap], rows, preferred_element_type=F32)
                amp_rows[swap, g * 48 : (g + 1) * 48, :] = picked.astype(BF16)

        def left_source(to, at):
            slot, j = to >> 3, to & 7
            pair, crossed = (slot - ta) & (half - 1), jnp.where(slot < ta + half, 0, 1)
            high = j * ta + 2 * (slot & (half - 1)) + jnp.where(slot < half, 0, 1)
            low = (8 + (j & 3)) * ta + 2 * pair + ((j >> 2) ^ crossed)
            return at == jnp.where(slot < ta, high, low)

        picks[...] = one_hot(picks.shape, left_source)

    def make_left(left_ref, block):
        at = pl.ds(pl.multiple_of(jnp.minimum(block, blocks - 1) * ta, ta), ta)
        rows = jnp.concatenate([ac[:, at, :].reshape(c_dev * ta, q) for ac in ac_refs])
        left_ref[...] = jnp.dot(picks[...], rows, preferred_element_type=F32).astype(BF16)

    def left_rows(left_ref):
        high, even = left_ref[: 8 * ta], left_ref[8 * ta : 8 * (ta + half)]
        return jnp.concatenate([high, even]), jnp.concatenate([high, left_ref[8 * (ta + half) :]])

    upper = lax.broadcasted_iota(jnp.int32, (half, 8, nb), 1) < 4

    def first(left, ints_ref, g):
        high, low = [], []
        for d in range(4 * g, 4 * g + 4):
            ints = lax.dot_general(
                left[d % 2], bd_refs[d // d_dev][d % d_dev], (((1,), (1,)), ((), ())),
                preferred_element_type=F32,
            )
            high.append(ints[: 8 * ta].reshape(ta, 8, nb))
            low.append(ints[8 * ta :].reshape(half, 8, nb))
        k = 48 * g
        for n in (0, 2):
            both = jnp.concatenate(high[n : n + 2], axis=1).astype(BF16)
            ints_ref[:, k + 8 * n : k + 8 * n + 16, :] = both
        even = [jnp.where(upper, low[n], low[n + 1]) for n in (0, 2)]
        odd = [jnp.where(upper, low[n + 1], low[n]) for n in (0, 2)]
        ints_ref[:half, k + 32 : k + 48, :] = jnp.concatenate(even, axis=1).astype(BF16)
        ints_ref[half:, k + 32 : k + 48, :] = jnp.concatenate(odd, axis=1).astype(BF16)

    def second(ints_ref, slot):
        out_ref[2 * (slot % half) + slot // half] = lax.dot_general(
            ints_ref[slot], amp_rows[slot // half], (((0,), (0,)), ((), ())),
            preferred_element_type=F32,
        )

    def both(done_ref, next_ref, left_ref, next_left):
        left = left_rows(left_ref)
        for g in range(groups):
            first(left, next_ref, g)
            if g == groups // 2:
                make_left(next_left, i + 1)
            for slot in range(g * ta // groups, (g + 1) * ta // groups):
                second(done_ref, slot)

    @pl.when(i == 0)
    def _():
        prepare()
        make_left(left_a, 0)
        left = left_rows(left_a)
        for g in range(groups):
            first(left, ints_a, g)
        make_left(left_b, 1)

    @pl.when((i % 2 == 1) & (i < blocks))
    def _():
        both(ints_a, ints_b, left_b, left_a)

    @pl.when((i % 2 == 0) & (i > 0) & (i < blocks))
    def _():
        both(ints_b, ints_a, left_a, left_b)

    @pl.when(i == blocks)
    def _():
        for slot in range(ta):
            second((ints_a, ints_b)[(blocks - 1) % 2], slot)


def ladder(bd_pieces, ac_pieces, amps):
    c_dev, na, q = ac_pieces[0].shape
    d_dev, nb, _ = bd_pieces[0].shape
    m_count, s_count, pairs = len(bd_pieces), len(ac_pieces), amps[0].shape[-1]
    ta = 16 if na % 16 == 0 else 8
    blocks = na // ta
    c_all = c_dev * s_count
    depth = m_count * d_dev * rounded_up(c_all, 16)
    if (m_count, d_dev, c_all, ta) == (8, 3, 12, 16):
        tight = m_count * d_dev * c_all
        scratch = [pltpu.VMEM((ta, tight, nb), BF16)] * 2 + [pltpu.VMEM((16 * ta, q), BF16)] * 2 + [
            pltpu.VMEM((depth, pairs), BF16),
            pltpu.VMEM((2, tight, pairs), BF16),
            pltpu.VMEM((16 * ta, c_all * ta), BF16),
        ]
        body, steps, limit = functools.partial(kernel, m_count, s_count, blocks), blocks + 1, 32
        at_out = lambda i: (jnp.maximum(i - 1, 0), 0, 0)
        in_specs = [pl.BlockSpec(memory_space=pltpu.VMEM)] * (m_count + s_count + len(amps))
    else:
        scratch = [pltpu.VMEM((ta, depth, nb), BF16), pltpu.VMEM((depth, pairs), BF16)]
        body, steps, limit = functools.partial(plain_kernel, m_count, s_count), blocks, 60
        at_out = lambda i: (i, 0, 0)
        whole = pl.Buffered(1)
        in_specs = (
            [pl.BlockSpec((d_dev, nb, q), lambda i: (0, 0, 0), pipeline_mode=whole)] * m_count
            + [pl.BlockSpec((c_dev, ta, q), lambda i: (0, i, 0))] * s_count
            + [pl.BlockSpec(amps[0].shape, lambda i: (0, 0), pipeline_mode=whole)] * len(amps)
        )
    return pl.pallas_call(
        body,
        grid=(steps,),
        in_specs=in_specs,
        out_specs=pl.BlockSpec((ta, nb, pairs), at_out),
        out_shape=jax.ShapeDtypeStruct((na, nb, pairs), F32),
        scratch_shapes=scratch,
        compiler_params=pltpu.CompilerParams(vmem_limit_bytes=limit << 20),
    )(*bd_pieces, *ac_pieces, *amps)


def body(n_row, n_col, fac_ac, fac_bd, amps):
    def send(x, to):
        return lax.ppermute(x, "row", [(i, to(i)) for i in range(n_row)])

    def flip(x):
        return send(x, lambda i: i ^ 1)

    def shift(x, s):
        to = (lambda i: i ^ s) if n_col & (n_col - 1) == 0 else (lambda i: (i + s) % n_col)
        return lax.ppermute(x, "col", [(i, to(i)) for i in range(n_col)])

    bd = jnp.transpose(fac_bd, (1, 0, 2))
    ac = jnp.transpose(fac_ac, (1, 0, 2))
    c_dev, d_dev, pairs = amps.shape
    c_pad = rounded_up(c_dev * n_col, 16)
    amp_cols = [amps] + [shift(amps, s) for s in range(1, n_col)]
    rows = jnp.concatenate(amp_cols)
    rows = jnp.pad(rows, ((0, c_pad - c_dev * n_col), (0, 0), (0, 0)))
    rows = jnp.transpose(rows, (1, 0, 2)).reshape(d_dev * c_pad, pairs)
    ac_pieces = [ac] + [shift(ac, s) for s in range(1, n_col)]
    rows = jnp.concatenate([rows, flip(rows)])
    masks = range(2, n_row, 2)
    amp_rows = [rows] + [send(rows, lambda i: i ^ m) for m in masks]
    if (n_row, d_dev, c_dev * n_col) != (8, 3, 12):
        bd_even = [bd] + [send(bd, lambda i: i ^ m) for m in masks]
        bd_pieces = [x for even in bd_even for x in (even, flip(even))]
        return ladder(bd_pieces, ac_pieces, amp_rows)

    over, then = (lambda i: i ^ (2 if i & 1 else 4)), (lambda i: i ^ (4 if i & 1 else 2))
    other = flip(bd)
    first, second = send(bd, over), send(bd, then)
    far = send(first, then)
    bd_pieces = [flip(other), other]
    ac_pieces[0] = flip(flip(ac))
    for piece in (first, second, far):
        bd_pieces += [piece, flip(piece)]
    return ladder(bd_pieces, ac_pieces, amp_rows)


def solution(mesh):
    n_row, n_col = mesh.shape["row"], mesh.shape["col"]
    in_specs = (P("row", "col", None), P("col", "row", None), P("col", "row", None))
    out_specs = P("row", "col", None)
    return jax.shard_map(
        functools.partial(body, n_row, n_col),
        mesh=mesh, in_specs=in_specs, out_specs=out_specs, check_vma=False,
    )
```
